32 devices in a mesh: groups: 2 (over y), seq: 16 (over z, x, core).
Axes of the slice: x: 2, y: 2, z: 4, core: 2. Of those that a mesh axis runs over, the one named last changes fastest.
Arguments:
- query_rows: bfloat16 [8192, 8, 128], P(('groups', 'seq')), parts along dimension 0, may hold values from -48 to 48
- key_rows: bfloat16 [8192, 8, 128], P(('groups', 'seq')), parts along dimension 0, may hold values from -7 to 7
- value_rows: bfloat16 [8192, 8, 128], P(('groups', 'seq')), parts along dimension 0, may hold values from -6 to 6
- out_grad: bfloat16 [8192, 8, 128], P(('groups', 'seq')), parts along dimension 0, may hold values from -6 to 6
Outputs:
- attended: bfloat16 [8192, 8, 128], P(('groups', 'seq')), parts along dimension 0
- query_grad: bfloat16 [8192, 8, 128], P(('groups', 'seq')), parts along dimension 0
- key_grad: bfloat16 [8192, 8, 128], P(('groups', 'seq')), parts along dimension 0
- value_grad: bfloat16 [8192, 8, 128], P(('groups', 'seq')), parts along dimension 0
The draws below stay inside these ranges and needn't reach their ends.
There are 2 independent parts, one for each index of `groups`. The reference program is written for one: setup_inputs(seed, part) draws one part's arguments, and reference() takes and returns one part's arrays. A program takes and returns all parts, laid end to end along the dimension named above; each array names one. Nothing has to cross between parts.
All inputs are finite; a program needn't handle non-finite values.
Results may differ from the reference program's by a relative error of at most 0.018.
Values may be sent and summed in bfloat16 or wider, within the bound.
A program may use at most 128 MiB of HBM per device.

```python
from functools import partial
import jax
import jax.numpy as jnp
from jax import lax

HEADS = 8
HDIM = 128
BLOCK = 128
TOKENS = 4096


def layered(key, stream):
    dims = (TOKENS, HEADS, HDIM)
    summed = jnp.zeros(dims, jnp.float32)
    top_exponent = TOKENS.bit_length() - 1
    for exponent in range(4, top_exponent - 2):
        run_shape = (TOKENS >> exponent, HEADS, HDIM)
        sub_key = jax.random.fold_in(key, stream + exponent)
        run_values = jax.random.truncated_normal(sub_key, -3.0, 3.0, run_shape, jnp.float32)
        summed = summed + jnp.repeat(run_values, 1 << exponent, axis=0)
    return summed


def drawn_noise(key, stream, spread, shaped):
    sub_key = jax.random.fold_in(key, stream)
    return spread * jax.random.truncated_normal(sub_key, -3.0, 3.0, shaped, jnp.float32)


def joint_pair(key):
    dims = (TOKENS, HEADS, HDIM)
    base_keys = drawn_noise(key, 11, 0.8, dims) + 0.35 * layered(key, 100)
    base_query = drawn_noise(key, 12, 2.0, dims) + layered(key, 200)
    return (jnp.clip(base_query, -48.0, 48.0), jnp.clip(base_keys, -7.0, 7.0))


def draw_query_rows(key, part):
    return joint_pair(key)[0].astype(jnp.bfloat16)


def draw_key_rows(key, part):
    return joint_pair(key)[1].astype(jnp.bfloat16)


def draw_value_rows(key, part):
    dims = (TOKENS, HEADS, HDIM)
    shift = jax.random.uniform(jax.random.fold_in(key, 21), (1, HEADS, HDIM), jnp.float32, -1.0, 1.0)
    field = drawn_noise(key, 22, 0.8, dims) + 0.3 * layered(key, 300) + shift
    return jnp.clip(field, -6.0, 6.0).astype(jnp.bfloat16)


def draw_out_grad(key, part):
    dims = (TOKENS, HEADS, HDIM)
    common = 0.8 * jax.random.truncated_normal(jax.random.fold_in(key, 31), -3.0, 3.0, (1, HEADS, HDIM), jnp.float32)
    field = drawn_noise(key, 32, 0.8, dims) + 0.25 * layered(key, 400) + common
    return jnp.clip(field, -6.0, 6.0).astype(jnp.bfloat16)


def setup_inputs(seed: int = 0, part: int = 0) -> dict:
    key_of = jax.random.split(jax.random.key(seed), 5)
    own_keys = jax.random.split(jax.random.fold_in(key_of[4], part), 5)
    query_rows = draw_query_rows(jax.random.fold_in(jax.random.fold_in(key_of[4], part), 71), part)
    key_rows = draw_key_rows(jax.random.fold_in(jax.random.fold_in(key_of[4], part), 71), part)
    value_rows = draw_value_rows(jax.random.fold_in(jax.random.fold_in(key_of[4], part), 71), part)
    out_grad = draw_out_grad(jax.random.fold_in(jax.random.fold_in(key_of[4], part), 71), part)
    return {"query_rows": query_rows, "key_rows": key_rows, "value_rows": value_rows, "out_grad": out_grad}


def keep_round(values):
    frozen = lax.stop_gradient(values)
    lowered = lax.optimization_barrier(frozen.astype(jnp.bfloat16))
    return values + (lowered.astype(values.dtype) - frozen)

def coarsen(fields, height):
    if height == 0:
        return fields
    row_count = fields.shape[0] >> height
    grouped = fields.reshape((row_count, 1 << height) + fields.shape[1:])
    return keep_round(lax.optimization_barrier(jnp.mean(grouped, axis=1)))

def block_term(weight, query_blocks, key_blocks, value_blocks):
    factor = query_blocks.shape[-1] ** (-0.5)
    scores = jnp.einsum('bqhd,bkhd->bqhk', query_blocks, key_blocks, precision=lax.Precision.HIGHEST) * factor
    row_max = lax.stop_gradient(lax.optimization_barrier(jnp.max(scores, axis=-1)))
    weights = jnp.exp(scores - row_max[..., None])
    denominator = weight * lax.optimization_barrier(jnp.sum(weights, axis=-1))
    numerator = weight * jnp.einsum('bqhk,bkhd->bqhd', keep_round(weights), value_blocks, precision=lax.Precision.HIGHEST)
    row_count = query_blocks.shape[0] * query_blocks.shape[1]
    return (row_max.reshape((row_count,) + row_max.shape[2:]), denominator.reshape((row_count,) + denominator.shape[2:]), numerator.reshape((row_count,) + numerator.shape[2:]))

def combine(earlier, second):
    row_max = jnp.maximum(earlier[0], second[0])
    scale_a = jnp.exp(earlier[0] - row_max)
    scale_b = jnp.exp(second[0] - row_max)
    return (row_max, scale_a * earlier[1] + scale_b * second[1], scale_a[..., None] * earlier[2] + scale_b[..., None] * second[2])

def upsample(summary):
    return tuple((jnp.repeat(entry, 2, axis=0) for entry in summary))

def flip_pairs(blocks):
    paired = blocks.reshape((blocks.shape[0] // 2, 2) + blocks.shape[1:])
    return paired[:, ::-1].reshape(blocks.shape)

def attend(query32, key32, value32):
    block_count = query32.shape[0] // BLOCK
    levels = block_count.bit_length() - 1
    summary = None
    for height in reversed(range(levels)):
        nblocks = block_count >> height
        block_shape = (nblocks, BLOCK) + query32.shape[1:]
        query_c = coarsen(query32, height).reshape(block_shape)
        keys_c = flip_pairs(coarsen(key32, height).reshape(block_shape))
        values_c = flip_pairs(coarsen(value32, height).reshape(block_shape))
        partial_term = jax.checkpoint(partial(block_term, float(1 << height)))(query_c, keys_c, values_c)
        summary = partial_term if summary is None else combine(upsample(summary), partial_term)
    block_shape = (block_count, BLOCK) + query32.shape[1:]
    diagonal = jax.checkpoint(partial(block_term, 1.0))(query32.reshape(block_shape), key32.reshape(block_shape), value32.reshape(block_shape))
    summary = combine(summary, diagonal)
    return summary[2] / summary[1][..., None]

def reference(query_rows, key_rows, value_rows, out_grad):
    attention, pullback = jax.vjp(attend, query_rows.astype(jnp.float32), key_rows.astype(jnp.float32), value_rows.astype(jnp.float32))
    grads = pullback(out_grad.astype(jnp.float32))
    return (attention.astype(jnp.bfloat16), grads[0].astype(jnp.bfloat16), grads[1].astype(jnp.bfloat16), grads[2].astype(jnp.bfloat16))
```

```python
from functools import partial

import jax
import jax.numpy as jnp
from jax import lax
from jax.experimental import pallas as pl
from jax.experimental.pallas import tpu as pltpu
from jax.sharding import PartitionSpec as P

BLOCK = 128
CHUNK = 16
F32 = jnp.float32
BF16 = jnp.bfloat16
MESH = pl.DeviceIdType.MESH


def bit_reversed(value, bits):
    return sum(((value >> bit) & 1) << (bits - 1 - bit) for bit in range(bits))


def load_rows(ref, head, heads, level):
    bits = max(4 - level, 0)
    parts = [
        ref[pl.ds(bit_reversed(b, bits) * heads + head, CHUNK, stride=heads << bits), :]
        for b in range(1 << bits)
    ]
    return parts[0] if len(parts) == 1 else jnp.concatenate(parts, 0)


def store_rows(ref, head, heads, level, values):
    bits = max(4 - level, 0)
    for b in range(1 << bits):
        ref[pl.ds(bit_reversed(b, bits) * heads + head, CHUNK, stride=heads << bits), :] = values[
            b * CHUNK : (b + 1) * CHUNK
        ]


def dot_nt(a, b):
    return lax.dot_general(a, b, (((1,), (1,)), ((), ())), preferred_element_type=F32)


def dot_nn(a, b):
    return lax.dot_general(a, b, (((1,), (0,)), ((), ())), preferred_element_type=F32)


def dot_tn(a, b):
    return lax.dot_general(a, b, (((0,), (0,)), ((), ())), preferred_element_type=F32)


def pair_sum(x):
    return jnp.sum(x.reshape((x.shape[0] // 2, 2) + x.shape[1:]), axis=1)


def repeat_rows(x, times):
    spread = jnp.broadcast_to(x[:, None], (x.shape[0], times) + x.shape[1:])
    return spread.reshape((x.shape[0] * times,) + x.shape[1:])


def kernel(levels, heads, width, rows, *refs):
    q_ref, k_ref, v_ref, g_ref, o_ref, dq_ref, dk_ref, dv_ref = refs[:8]
    (q32, k32, v32, g32, att32, tops, high, p0, num0, m0, l0, c0, d0) = refs[8:21]
    (sem_out, sem_in, sem_fwd_out, sem_fwd_in) = refs[21:25]
    (sem_half_out, sem_half_in, sem_back_out, sem_back_in) = refs[25:29]
    per = levels - 1
    cut = 29
    groups = [dict(zip(range(1, levels), refs[cut + i * per : cut + (i + 1) * per])) for i in range(7)]
    ql, own, got, kv32, give, gain, total = groups
    back = dict(zip(range(1, levels), refs[cut + 7 * per : cut + 8 * per]))
    factor = width ** (-0.5)
    remote = list(range(1, levels))
    wide = [level for level in remote if level >= 2]
    chunks = rows // CHUNK
    half = BLOCK // 2

    me = lax.axis_index("seq")
    core = me % 2
    sibling = me + 1 - 2 * core

    def partners(level):
        span = 1 << (level - 1)
        block = me // span
        base = (block + 1 - 2 * (block % 2)) * span
        return [base + 2 * j + core for j in range(span // 2)]

    def place(level):
        return (me % (1 << (level - 1))) // 2

    barrier = pltpu.get_barrier_semaphore()
    peers = [sibling] + [peer for level in wide for peer in partners(level)]
    for peer in peers:
        pl.semaphore_signal(barrier, inc=1, device_id={"seq": peer}, device_id_type=MESH)

    def remote_copy(src, dst, send, recv, peer):
        return pltpu.make_async_remote_copy(
            src_ref=src, dst_ref=dst, send_sem=send, recv_sem=recv,
            device_id={"seq": peer}, device_id_type=MESH,
        )

    def prepare_kv(i, carry):
        for which, (ref, store) in enumerate(((k_ref, k32), (v_ref, v32))):
            x = ref[pl.ds(i * CHUNK, CHUNK)].astype(F32)
            store[pl.ds(i * CHUNK * heads, CHUNK * heads), :] = x.reshape(CHUNK * heads, width)
            for level in range(1, min(levels, 5)):
                x = pair_sum(x)
                n = CHUNK >> level
                own[level][which, pl.ds(i * n, n)] = (x * 0.5**level).astype(BF16)
            if levels > 5:
                tops[which, pl.ds(i, 1)] = x
        return carry

    lax.fori_loop(0, chunks, prepare_kv, 0)
    for which in range(2):
        if levels > 5:
            x = tops[which]
            for level in range(5, levels):
                x = pair_sum(x)
                own[level][which] = (x * 0.5**level).astype(BF16)

    pl.semaphore_wait(barrier, len(peers))
    sends = []
    slot = 0
    for level in sorted(wide, reverse=True):
        n = rows >> level
        at = place(level) * n
        for peer in partners(level):
            sends.append(
                remote_copy(
                    own[level], got[level].at[core, :, pl.ds(at, n)],
                    sem_out.at[slot], sem_in.at[level], peer,
                )
            )
            sends[-1].start()
            slot += 1
    first = remote_copy(own[1], got[1].at[0], sem_out.at[slot], sem_in.at[1], sibling)
    first.start()

    def prepare_q(i, carry):
        x = q_ref[pl.ds(i * CHUNK, CHUNK)].astype(F32)
        q32[pl.ds(i * CHUNK * heads, CHUNK * heads), :] = x.reshape(CHUNK * heads, width)
        for level in range(1, min(levels, 5)):
            x = pair_sum(x)
            n = CHUNK >> level
            lowered = (x * 0.5**level).astype(BF16).astype(F32)
            ql[level][pl.ds(i * n * heads, n * heads), :] = lowered.reshape(n * heads, width)
        if levels > 5:
            tops[2, pl.ds(i, 1)] = x
        g = g_ref[pl.ds(i * CHUNK, CHUNK)].astype(F32)
        g32[pl.ds(i * CHUNK * heads, CHUNK * heads), :] = g.reshape(CHUNK * heads, width)
        return carry

    lax.fori_loop(0, chunks, prepare_q, 0)
    if levels > 5:
        x = tops[2]
        for level in range(5, levels):
            x = pair_sum(x)
            lowered = repeat_rows((x * 0.5**level).astype(BF16).astype(F32), 1 << (level - 4))
            ql[level][...] = lowered.reshape(CHUNK * heads, width)

    def near_forward(h, carry):
        q = load_rows(q32, h, heads, 0).astype(BF16)
        k = k32[pl.ds(h, rows, stride=heads), :].astype(BF16)
        v = v32[pl.ds(h, rows, stride=heads), :].astype(BF16)
        s = dot_nt(q, k) * factor
        m = jnp.max(s, axis=1, keepdims=True)
        p = jnp.exp(s - m)
        p0[h] = p
        m0[h] = m
        l0[h] = jnp.sum(p, axis=1, keepdims=True)
        num0[h] = dot_nn(p.astype(BF16), v)
        return carry

    lax.fori_loop(0, heads, near_forward, 0)

    forwards = {}
    for level in sorted(wide, reverse=True):
        mine = got[level].at[core]
        remote_copy(mine, mine, sem_out.at[0], sem_in.at[level], sibling).wait_recv()
        forwards[level] = remote_copy(
            mine, mine, sem_fwd_out.at[level], sem_fwd_in.at[level], sibling
        )
        forwards[level].start()
    first.wait_recv()

    def widen(level):
        parts = got[level].shape[0]
        depth = BLOCK // parts

        def body(i, carry):
            n = depth // 8
            for part in range(parts):
                for which in range(2):
                    x = got[level][part, which, pl.ds(i * n, n)].astype(F32)
                    kv32[level][which, pl.ds((part * depth + i * n) * heads, n * heads), :] = x.reshape(
                        n * heads, width
                    )
            return carry

        lax.fori_loop(0, 8, body, 0)

    widen(1)
    for level in sorted(wide, reverse=True):
        other = got[level].at[1 - core]
        remote_copy(other, other, sem_fwd_out.at[level], sem_fwd_in.at[level], sibling).wait_recv()
        widen(level)

    def far(h, carry):
        m_all = den = num = None
        kept = {}
        for level in reversed(remote):
            q = load_rows(ql[level], h, heads, level).astype(BF16)
            k = kv32[level][0, pl.ds(h, BLOCK, stride=heads), :].astype(BF16)
            v = kv32[level][1, pl.ds(h, BLOCK, stride=heads), :].astype(BF16)
            s = dot_nt(q, k) * factor
            m = jnp.max(s, axis=1, keepdims=True)
            p = jnp.exp(s - m)
            pb = p.astype(BF16)
            weight = float(1 << level)
            den_l = jnp.sum(p, axis=1, keepdims=True)
            num_l = dot_nn(pb, v)
            if m_all is None:
                scale_a, scale_b = None, jnp.full(m.shape, weight, F32)
                m_all, den, num = m, den_l * weight, num_l * weight
            else:
                if m_all.shape[0] < m.shape[0]:
                    m_all, den, num = (jnp.concatenate([x, x], 0) for x in (m_all, den, num))
                top = jnp.maximum(m_all, m)
                scale_a = jnp.exp(m_all - top)
                scale_b = jnp.exp(m - top) * weight
                m_all = top
                den = scale_a * den + scale_b * den_l
                num = scale_a * num + scale_b * num_l
            kept[level] = (q, k, v, p, pb, scale_a, scale_b)
        m = m0[h]
        m_all, den, num = (jnp.concatenate([x, x], 0) for x in (m_all, den, num))
        top = jnp.maximum(m_all, m)
        scale_a = jnp.exp(m_all - top)
        scale_b = jnp.exp(m - top)
        den = scale_a * den + scale_b * l0[h]
        num = scale_a * num + scale_b * num0[h]
        inverse = 1.0 / den
        att = num * inverse
        store_rows(att32, h, heads, 0, att)
        g = load_rows(g32, h, heads, 0)
        d = jnp.sum(g * att, axis=1, keepdims=True)
        c0[h] = scale_b * inverse
        d0[h] = d
        scale = scale_a * inverse
        up, up_d = g * scale, d * scale
        for level in remote:
            q, k, v, p, pb, scale_a, scale_b = kept[level]
            if up.shape[0] > q.shape[0]:
                n = q.shape[0]
                up, up_d = up[:n] + up[n:], up_d[:n] + up_d[n:]
            gb = (up * scale_b).astype(BF16)
            ds = (p * (dot_nt(gb, v) - up_d * scale_b) * factor).astype(BF16)
            store_rows(ql[level], h, heads, level, dot_nn(ds, k))
            kv32[level][0, pl.ds(h, BLOCK, stride=heads), :] = dot_tn(ds, q)
            kv32[level][1, pl.ds(h, BLOCK, stride=heads), :] = dot_tn(pb, gb)
            if scale_a is not None:
                up, up_d = up * scale_a, up_d * scale_a
        return carry

    lax.fori_loop(0, heads, far, 0)

    halves = {}
    for level in sorted(wide, reverse=True):

        def narrow(i, carry, level=level):
            n = half // 4
            for which in range(2):
                x = kv32[level][which, pl.ds(((1 - core) * half + i * n) * heads, n * heads), :]
                give[level][which, pl.ds(i * n, n)] = x.reshape(n, heads, width).astype(BF16)
            return carry

        lax.fori_loop(0, 4, narrow, 0)
        halves[level] = remote_copy(
            give[level], gain[level], sem_half_out.at[level], sem_half_in.at[level], sibling
        )
        halves[level].start()

    def narrow_first(i, carry):
        n = BLOCK // 8
        for which in range(2):
            x = kv32[1][which, pl.ds(i * n * heads, n * heads), :]
            give[1][which, pl.ds(i * n, n)] = x.reshape(n, heads, width).astype(BF16)
        return carry

    lax.fori_loop(0, 8, narrow_first, 0)
    first_back = remote_copy(
        give[1], back[1].at[0], sem_half_out.at[1], sem_back_in.at[1], sibling
    )
    first_back.start()

    returns = []
    slot = 0
    for level in sorted(wide, reverse=True):
        halves[level].wait_recv()

        def add(i, carry, level=level):
            n = half // 4
            for which in range(2):
                x = kv32[level][which, pl.ds((core * half + i * n) * heads, n * heads), :]
                y = gain[level][which, pl.ds(i * n, n)].astype(F32)
                total[level][which, pl.ds(i * n, n)] = (x.reshape(n, heads, width) + y).astype(BF16)
            return carry

        lax.fori_loop(0, 4, add, 0)
        n = rows >> level
        for j, peer in enumerate(partners(level)):
            returns.append(
                remote_copy(
                    total[level].at[:, pl.ds(j * n, n)], back[level].at[place(level)],
                    sem_back_out.at[slot], sem_back_in.at[level], peer,
                )
            )
            returns[-1].start()
            slot += 1

    def near_backward(h, carry):
        q = load_rows(q32, h, heads, 0).astype(BF16)
        g = load_rows(g32, h, heads, 0).astype(BF16)
        k = k32[pl.ds(h, rows, stride=heads), :].astype(BF16)
        v = v32[pl.ds(h, rows, stride=heads), :].astype(BF16)
        p = p0[h] * c0[h]
        ds = (p * (dot_nt(g, v) - d0[h]) * factor).astype(BF16)
        store_rows(q32, h, heads, 0, dot_nn(ds, k))
        k32[pl.ds(h, rows, stride=heads), :] = dot_tn(ds, q)
        v32[pl.ds(h, rows, stride=heads), :] = dot_tn(p.astype(BF16), g)
        return carry

    lax.fori_loop(0, heads, near_backward, 0)

    low = range(1, min(levels, 5))

    def finish_q(i, carry):
        o = att32[pl.ds(i * CHUNK * heads, CHUNK * heads), :]
        o_ref[pl.ds(i * CHUNK, CHUNK)] = o.reshape(CHUNK, heads, width).astype(BF16)
        extra = high[0, pl.ds(i, 1)] if levels > 5 else None
        for level in reversed(low):
            n = CHUNK >> level
            x = ql[level][pl.ds(i * n * heads, n * heads), :].reshape(n, heads, width) * 0.5**level
            extra = x if extra is None else x + repeat_rows(extra, n // extra.shape[0])
        x = q32[pl.ds(i * CHUNK * heads, CHUNK * heads), :].reshape(CHUNK, heads, width)
        if extra is not None:
            x = x + repeat_rows(extra, 2)
        dq_ref[pl.ds(i * CHUNK, CHUNK)] = x.astype(BF16)
        return carry

    if levels > 5:
        total_q = jnp.zeros((CHUNK, heads, width), F32)
        for level in range(5, levels):
            x = ql[level][...].reshape(CHUNK, heads, width)
            for _ in range(level - 4):
                x = pair_sum(x)
            total_q = total_q + repeat_rows(x * 0.5**level, 1 << (level - 4))
        high[0] = total_q
    lax.fori_loop(0, chunks, finish_q, 0)

    first_back.wait_recv()
    for level in wide:
        remote_copy(
            back[level], back[level], sem_back_out.at[0], sem_back_in.at[level], sibling
        ).wait_recv()

    if levels > 5:
        for which in range(2):
            total_k = jnp.zeros((CHUNK, heads, width), F32)
            for level in range(5, levels):
                x = back[level][0, which].astype(F32)
                for j in range(1, back[level].shape[0]):
                    x = x + back[level][j, which].astype(F32)
                total_k = total_k + repeat_rows(x * 0.5**level, 1 << (level - 4))
            high[1 + which] = total_k

    def finish_kv(i, carry):
        for which, (near, out) in enumerate(((k32, dk_ref), (v32, dv_ref))):
            extra = high[1 + which, pl.ds(i, 1)] if levels > 5 else None
            for level in reversed(low):
                n = CHUNK >> level
                x = back[level][0, which, pl.ds(i * n, n)].astype(F32)
                for j in range(1, back[level].shape[0]):
                    x = x + back[level][j, which, pl.ds(i * n, n)].astype(F32)
                x = x * 0.5**level
                extra = x if extra is None else x + repeat_rows(extra, n // extra.shape[0])
            x = near[pl.ds(i * CHUNK * heads, CHUNK * heads), :].reshape(CHUNK, heads, width)
            if extra is not None:
                x = x + repeat_rows(extra, 2)
            out[pl.ds(i * CHUNK, CHUNK)] = x.astype(BF16)
        return carry

    lax.fori_loop(0, chunks, finish_kv, 0)

    for copy in sends + [first] + list(forwards.values()) + list(halves.values()):
        copy.wait_send()
    for copy in [first_back] + returns:
        copy.wait_send()


def on_device(query_rows, key_rows, value_rows, out_grad):
    rows, heads, width = query_rows.shape
    devices = lax.axis_size("seq")
    levels = (rows * devices // BLOCK).bit_length() - 1
    remote = range(1, levels)
    wide = range(2, levels)
    copies = 1 + sum(1 << (level - 2) for level in wide)
    half = BLOCK // 2

    def kept(level):
        return max(rows >> level, CHUNK)

    flat = (rows * heads, width)
    dma = pltpu.SemaphoreType.DMA
    scratch = [pltpu.VMEM(flat, F32) for _ in range(5)]
    scratch += [pltpu.VMEM((3, CHUNK, heads, width), F32) for _ in range(2)]
    scratch += [pltpu.VMEM((heads, rows, rows), F32), pltpu.VMEM((heads, rows, width), F32)]
    scratch += [pltpu.VMEM((heads, rows, 1), F32) for _ in range(4)]
    scratch += [dma((copies,)), dma((levels,)), dma((levels,)), dma((levels,))]
    scratch += [dma((levels,)), dma((levels,)), dma((copies,)), dma((levels,))]
    scratch += [pltpu.VMEM((kept(level) * heads, width), F32) for level in remote]
    scratch += [pltpu.VMEM((2, rows >> level, heads, width), BF16) for level in remote]
    scratch += [
        pltpu.VMEM((1, 2, BLOCK, heads, width) if level == 1 else (2, 2, half, heads, width), BF16)
        for level in remote
    ]
    scratch += [pltpu.VMEM((2, BLOCK * heads, width), F32) for level in remote]
    scratch += [
        pltpu.VMEM((2, BLOCK if level == 1 else half, heads, width), BF16) for level in remote
    ]
    for _ in range(2):
        scratch += [
            pltpu.VMEM((2, CHUNK if level == 1 else half, heads, width), BF16) for level in remote
        ]
    scratch += [
        pltpu.VMEM((max(1 << level >> 2, 1), 2, rows >> level, heads, width), BF16)
        for level in remote
    ]
    vmem = pl.BlockSpec(memory_space=pltpu.VMEM)
    out = jax.ShapeDtypeStruct(query_rows.shape, BF16)
    return pl.pallas_call(
        partial(kernel, levels, heads, width, rows),
        out_shape=(out, out, out, out),
        in_specs=[vmem] * 4,
        out_specs=(vmem,) * 4,
        scratch_shapes=scratch,
        compiler_params=pltpu.CompilerParams(
            collective_id=0, has_side_effects=True, vmem_limit_bytes=58 << 20
        ),
    )(query_rows, key_rows, value_rows, out_grad)


def solution(mesh):
    spec = P(("groups", "seq"), None, None)
    return jax.shard_map(
        on_device,
        mesh=mesh,
        in_specs=(spec,) * 4,
        out_specs=(spec,) * 4,
        check_vma=False,
    )
```

```python
from functools import partial

import jax
import jax.numpy as jnp
from jax import lax
from jax.experimental import pallas as pl
from jax.experimental.pallas import tpu as pltpu
from jax.sharding import PartitionSpec as P

BLOCK = 128
CHUNK = 16
F32 = jnp.float32
BF16 = jnp.bfloat16
MESH = pl.DeviceIdType.MESH


def bit_reversed(value, bits):
    return sum(((value >> bit) & 1) << (bits - 1 - bit) for bit in range(bits))


def load_rows(ref, head, heads, level):
    bits = max(4 - level, 0)
    parts = [
        ref[pl.ds(bit_reversed(b, bits) * heads + head, CHUNK, stride=heads << bits), :]
        for b in range(1 << bits)
    ]
    return parts[0] if len(parts) == 1 else jnp.concatenate(parts, 0)


def store_rows(ref, head, heads, level, values):
    bits = max(4 - level, 0)
    for b in range(1 << bits):
        ref[pl.ds(bit_reversed(b, bits) * heads + head, CHUNK, stride=heads << bits), :] = values[
            b * CHUNK : (b + 1) * CHUNK
        ]


def dot_nt(a, b):
    return lax.dot_general(a, b, (((1,), (1,)), ((), ())), preferred_element_type=F32)


def dot_nn(a, b):
    return lax.dot_general(a, b, (((1,), (0,)), ((), ())), preferred_element_type=F32)


def dot_tn(a, b):
    return lax.dot_general(a, b, (((0,), (0,)), ((), ())), preferred_element_type=F32)


def pair_sum(x):
    return jnp.sum(x.reshape((x.shape[0] // 2, 2) + x.shape[1:]), axis=1)


def repeat_rows(x, times):
    spread = jnp.broadcast_to(x[:, None], (x.shape[0], times) + x.shape[1:])
    return spread.reshape((x.shape[0] * times,) + x.shape[1:])


def kernel(levels, heads, width, rows, *refs):
    q_ref, k_ref, v_ref, g_ref, o_ref, dq_ref, dk_ref, dv_ref = refs[:8]
    (q32, k32, v32, g32, att32, tops, high, p0, num0, m0, l0, c0, d0) = refs[8:21]
    (sem_out, sem_in, sem_fwd_out, sem_fwd_in) = refs[21:25]
    (sem_half_out, sem_half_in, sem_back_out, sem_back_in) = refs[25:29]
    per = levels - 1
    cut = 29
    groups = [dict(zip(range(1, levels), refs[cut + i * per : cut + (i + 1) * per])) for i in range(14)]
    ql, own, got, kv32, give, gain, total, back, pf, mf, lf, numf, gf, df = groups
    factor = width ** (-0.5)
    remote = list(range(1, levels))
    wide = [level for level in remote if level >= 2]
    chunks = rows // CHUNK
    half = BLOCK // 2

    me = lax.axis_index("seq")
    core = me % 2
    sibling = me + 1 - 2 * core

    def partners(level):
        span = 1 << (level - 1)
        block = me // span
        base = (block + 1 - 2 * (block % 2)) * span
        return [base + 2 * j + core for j in range(span // 2)]

    def place(level):
        return (me % (1 << (level - 1))) // 2

    barrier = pltpu.get_barrier_semaphore()
    peers = [sibling] + [peer for level in wide for peer in partners(level)]
    for peer in peers:
        pl.semaphore_signal(barrier, inc=1, device_id={"seq": peer}, device_id_type=MESH)

    def remote_copy(src, dst, send, recv, peer):
        return pltpu.make_async_remote_copy(
            src_ref=src, dst_ref=dst, send_sem=send, recv_sem=recv,
            device_id={"seq": peer}, device_id_type=MESH,
        )

    def prepare_kv(i, carry):
        for which, (ref, store) in enumerate(((k_ref, k32), (v_ref, v32))):
            x = ref[pl.ds(i * CHUNK, CHUNK)].astype(F32)
            store[pl.ds(i * CHUNK * heads, CHUNK * heads), :] = x.reshape(CHUNK * heads, width)
            for level in range(1, min(levels, 5)):
                x = pair_sum(x)
                n = CHUNK >> level
                own[level][which, pl.ds(i * n, n)] = (x * 0.5**level).astype(BF16)
            if levels > 5:
                tops[which, pl.ds(i, 1)] = x
        return carry

    lax.fori_loop(0, chunks, prepare_kv, 0)
    for which in range(2):
        if levels > 5:
            x = tops[which]
            for level in range(5, levels):
                x = pair_sum(x)
                own[level][which] = (x * 0.5**level).astype(BF16)

    pl.semaphore_wait(barrier, len(peers))
    sends = []
    slot = 0
    for level in sorted(wide, reverse=True):
        n = rows >> level
        at = place(level) * n
        for peer in partners(level):
            sends.append(
                remote_copy(
                    own[level], got[level].at[core, :, pl.ds(at, n)],
                    sem_out.at[slot], sem_in.at[level], peer,
                )
            )
            sends[-1].start()
            slot += 1
    first = remote_copy(own[1], got[1].at[0], sem_out.at[slot], sem_in.at[1], sibling)
    first.start()

    def prepare_q(i, carry):
        x = q_ref[pl.ds(i * CHUNK, CHUNK)].astype(F32)
        q32[pl.ds(i * CHUNK * heads, CHUNK * heads), :] = x.reshape(CHUNK * heads, width)
        for level in range(1, min(levels, 5)):
            x = pair_sum(x)
            n = CHUNK >> level
            lowered = (x * 0.5**level).astype(BF16).astype(F32)
            ql[level][pl.ds(i * n * heads, n * heads), :] = lowered.reshape(n * heads, width)
        if levels > 5:
            tops[2, pl.ds(i, 1)] = x
        g = g_ref[pl.ds(i * CHUNK, CHUNK)].astype(F32)
        g32[pl.ds(i * CHUNK * heads, CHUNK * heads), :] = g.reshape(CHUNK * heads, width)
        return carry

    lax.fori_loop(0, chunks, prepare_q, 0)
    if levels > 5:
        x = tops[2]
        for level in range(5, levels):
            x = pair_sum(x)
            lowered = repeat_rows((x * 0.5**level).astype(BF16).astype(F32), 1 << (level - 4))
            ql[level][...] = lowered.reshape(CHUNK * heads, width)

    def in_groups(count, body):
        def step(i, carry):
            body([i * count + j for j in range(count)])
            return carry

        lax.fori_loop(0, heads // count, step, 0)

    def near_forward(hs):
        q = [load_rows(q32, h, heads, 0).astype(BF16) for h in hs]
        k = [k32[pl.ds(h, rows, stride=heads), :].astype(BF16) for h in hs]
        v = [v32[pl.ds(h, rows, stride=heads), :].astype(BF16) for h in hs]
        s = [dot_nt(x, y) * factor for x, y in zip(q, k)]
        m = [jnp.max(x, axis=1, keepdims=True) for x in s]
        p = [jnp.exp(x - y) for x, y in zip(s, m)]
        num = [dot_nn(x.astype(BF16), y) for x, y in zip(p, v)]
        for h, x, y, z in zip(hs, p, m, num):
            p0[h] = x
            m0[h] = y
            l0[h] = jnp.sum(x, axis=1, keepdims=True)
            num0[h] = z

    def far_forward(level, hs):
        q = [load_rows(ql[level], h, heads, level).astype(BF16) for h in hs]
        k = [kv32[level][0, pl.ds(h, BLOCK, stride=heads), :].astype(BF16) for h in hs]
        v = [kv32[level][1, pl.ds(h, BLOCK, stride=heads), :].astype(BF16) for h in hs]
        s = [dot_nt(x, y) * factor for x, y in zip(q, k)]
        m = [jnp.max(x, axis=1, keepdims=True) for x in s]
        p = [jnp.exp(x - y) for x, y in zip(s, m)]
        num = [dot_nn(x.astype(BF16), y) for x, y in zip(p, v)]
        for h, x, y, z in zip(hs, p, m, num):
            pf[level][h] = x
            mf[level][h] = y
            lf[level][h] = jnp.sum(x, axis=1, keepdims=True)
            numf[level][h] = z

    in_groups(2, near_forward)

    def widen(level):
        parts = got[level].shape[0]
        depth = BLOCK // parts

        def body(i, carry):
            n = depth // 8
            for part in range(parts):
                for which in range(2):
                    x = got[level][part, which, pl.ds(i * n, n)].astype(F32)
                    kv32[level][which, pl.ds((part * depth + i * n) * heads, n * heads), :] = x.reshape(
                        n * heads, width
                    )
            return carry

        lax.fori_loop(0, 8, body, 0)

    def take(level):
        other = got[level].at[1 - core]
        remote_copy(other, other, sem_fwd_out.at[level], sem_fwd_in.at[level], sibling).wait_recv()
        widen(level)
        in_groups(4, partial(far_forward, level))

    first.wait_recv()
    widen(1)
    in_groups(4, partial(far_forward, 1))

    forwards = {}
    order = sorted(wide, reverse=True)
    for step, level in enumerate(order):
        mine = got[level].at[core]
        remote_copy(mine, mine, sem_out.at[0], sem_in.at[level], sibling).wait_recv()
        forwards[level] = remote_copy(
            mine, mine, sem_fwd_out.at[level], sem_fwd_in.at[level], sibling
        )
        forwards[level].start()
        if step:
            take(order[step - 1])
    if order:
        take(order[-1])

    def merge(hs):
        for h in hs:
            state = None
            scales = {}
            for level in reversed(range(levels)):
                if level:
                    m, den_l, num_l = mf[level][h], lf[level][h], numf[level][h]
                else:
                    m, den_l, num_l = m0[h], l0[h], num0[h]
                weight = float(1 << level)
                if state is None:
                    scale_a, scale_b = None, jnp.full(m.shape, weight, F32)
                    state = (m, den_l * weight, num_l * weight)
                else:
                    if state[0].shape[0] < m.shape[0]:
                        state = tuple(jnp.concatenate([x, x], 0) for x in state)
                    top = jnp.maximum(state[0], m)
                    scale_a = jnp.exp(state[0] - top)
                    scale_b = jnp.exp(m - top) * weight
                    state = (
                        top,
                        scale_a * state[1] + scale_b * den_l,
                        scale_a * state[2] + scale_b * num_l,
                    )
                scales[level] = (scale_a, scale_b)
            inverse = 1.0 / state[1]
            att = state[2] * inverse
            store_rows(att32, h, heads, 0, att)
            g = load_rows(g32, h, heads, 0)
            d = jnp.sum(g * att, axis=1, keepdims=True)
            c0[h] = scales[0][1] * inverse
            d0[h] = d
            if levels == 1:
                continue
            scale = scales[0][0] * inverse
            up, up_d = g * scale, d * scale
            for level in remote:
                scale_a, scale_b = scales[level]
                if up.shape[0] > scale_b.shape[0]:
                    n = scale_b.shape[0]
                    up, up_d = up[:n] + up[n:], up_d[:n] + up_d[n:]
                gf[level][h] = (up * scale_b).astype(BF16)
                df[level][h] = up_d * scale_b
                if scale_a is not None:
                    up, up_d = up * scale_a, up_d * scale_a

    in_groups(2, merge)

    def far_backward(level, hs):
        q = [load_rows(ql[level], h, heads, level).astype(BF16) for h in hs]
        k = [kv32[level][0, pl.ds(h, BLOCK, stride=heads), :].astype(BF16) for h in hs]
        v = [kv32[level][1, pl.ds(h, BLOCK, stride=heads), :].astype(BF16) for h in hs]
        p = [pf[level][h] for h in hs]
        g = [gf[level][h] for h in hs]
        d = [df[level][h] for h in hs]
        dp = [dot_nt(x, y) for x, y in zip(g, v)]
        ds = [(x * (y - z) * factor).astype(BF16) for x, y, z in zip(p, dp, d)]
        dv = [dot_tn(x.astype(BF16), y) for x, y in zip(p, g)]
        dq = [dot_nn(x, y) for x, y in zip(ds, k)]
        dk = [dot_tn(x, y) for x, y in zip(ds, q)]
        for h, x, y, z in zip(hs, dq, dk, dv):
            store_rows(ql[level], h, heads, level, x)
            kv32[level][0, pl.ds(h, BLOCK, stride=heads), :] = y
            kv32[level][1, pl.ds(h, BLOCK, stride=heads), :] = z

    halves = {}
    returns = []

    def leave(level):
        in_groups(4, partial(far_backward, level))

        def narrow(i, carry):
            n = half // 4
            for which in range(2):
                x = kv32[level][which, pl.ds(((1 - core) * half + i * n) * heads, n * heads), :]
                give[level][which, pl.ds(i * n, n)] = x.reshape(n, heads, width).astype(BF16)
            return carry

        lax.fori_loop(0, 4, narrow, 0)
        halves[level] = remote_copy(
            give[level], gain[level], sem_half_out.at[level], sem_half_in.at[level], sibling
        )
        halves[level].start()

    def pass_on(level):
        halves[level].wait_recv()

        def add(i, carry):
            n = half // 4
            for which in range(2):
                x = kv32[level][which, pl.ds((core * half + i * n) * heads, n * heads), :]
                y = gain[level][which, pl.ds(i * n, n)].astype(F32)
                total[level][which, pl.ds(i * n, n)] = (x.reshape(n, heads, width) + y).astype(BF16)
            return carry

        lax.fori_loop(0, 4, add, 0)
        n = rows >> level
        for j, peer in enumerate(partners(level)):
            returns.append(
                remote_copy(
                    total[level].at[:, pl.ds(j * n, n)], back[level].at[place(level)],
                    sem_back_out.at[len(returns)], sem_back_in.at[level], peer,
                )
            )
            returns[-1].start()

    for step, level in enumerate(wide):
        leave(level)
        if step:
            pass_on(wide[step - 1])
    in_groups(4, partial(far_backward, 1))

    def narrow_first(i, carry):
        n = BLOCK // 8
        for which in range(2):
            x = kv32[1][which, pl.ds(i * n * heads, n * heads), :]
            give[1][which, pl.ds(i * n, n)] = x.reshape(n, heads, width).astype(BF16)
        return carry

    if wide:
        pass_on(wide[-1])
    lax.fori_loop(0, 8, narrow_first, 0)
    first_back = remote_copy(
        give[1], back[1].at[0], sem_half_out.at[1], sem_back_in.at[1], sibling
    )
    first_back.start()

    def near_backward(hs):
        q = [load_rows(q32, h, heads, 0).astype(BF16) for h in hs]
        g = [load_rows(g32, h, heads, 0).astype(BF16) for h in hs]
        k = [k32[pl.ds(h, rows, stride=heads), :].astype(BF16) for h in hs]
        v = [v32[pl.ds(h, rows, stride=heads), :].astype(BF16) for h in hs]
        p = [p0[h] * c0[h] for h in hs]
        dp = [dot_nt(x, y) for x, y in zip(g, v)]
        ds = [(x * (y - d0[h]) * factor).astype(BF16) for x, y, h in zip(p, dp, hs)]
        dv = [dot_tn(x.astype(BF16), y) for x, y in zip(p, g)]
        dq = [dot_nn(x, y) for x, y in zip(ds, k)]
        dk = [dot_tn(x, y) for x, y in zip(ds, q)]
        for h, x, y, z in zip(hs, dq, dk, dv):
            store_rows(q32, h, heads, 0, x)
            k32[pl.ds(h, rows, stride=heads), :] = y
            v32[pl.ds(h, rows, stride=heads), :] = z

    in_groups(2, near_backward)

    low = range(1, min(levels, 5))

    def finish_q(i, carry):
        o = att32[pl.ds(i * CHUNK * heads, CHUNK * heads), :]
        o_ref[pl.ds(i * CHUNK, CHUNK)] = o.reshape(CHUNK, heads, width).astype(BF16)
        extra = high[0, pl.ds(i, 1)] if levels > 5 else None
        for level in reversed(low):
            n = CHUNK >> level
            x = ql[level][pl.ds(i * n * heads, n * heads), :].reshape(n, heads, width) * 0.5**level
            extra = x if extra is None else x + repeat_rows(extra, n // extra.shape[0])
        x = q32[pl.ds(i * CHUNK * heads, CHUNK * heads), :].reshape(CHUNK, heads, width)
        if extra is not None:
            x = x + repeat_rows(extra, 2)
        dq_ref[pl.ds(i * CHUNK, CHUNK)] = x.astype(BF16)
        return carry

    if levels > 5:
        total_q = jnp.zeros((CHUNK, heads, width), F32)
        for level in range(5, levels):
            x = ql[level][...].reshape(CHUNK, heads, width)
            for _ in range(level - 4):
                x = pair_sum(x)
            total_q = total_q + repeat_rows(x * 0.5**level, 1 << (level - 4))
        high[0] = total_q
    lax.fori_loop(0, chunks, finish_q, 0)

    first_back.wait_recv()
    for level in wide:
        remote_copy(
            back[level], back[level], sem_back_out.at[0], sem_back_in.at[level], sibling
        ).wait_recv()

    if levels > 5:
        for which in range(2):
            total_k = jnp.zeros((CHUNK, heads, width), F32)
            for level in range(5, levels):
                x = back[level][0, which].astype(F32)
                for j in range(1, back[level].shape[0]):
                    x = x + back[level][j, which].astype(F32)
                total_k = total_k + repeat_rows(x * 0.5**level, 1 << (level - 4))
            high[1 + which] = total_k

    def finish_kv(i, carry):
        for which, (near, out) in enumerate(((k32, dk_ref), (v32, dv_ref))):
            extra = high[1 + which, pl.ds(i, 1)] if levels > 5 else None
            for level in reversed(low):
                n = CHUNK >> level
                x = back[level][0, which, pl.ds(i * n, n)].astype(F32)
                for j in range(1, back[level].shape[0]):
                    x = x + back[level][j, which, pl.ds(i * n, n)].astype(F32)
                x = x * 0.5**level
                extra = x if extra is None else x + repeat_rows(extra, n // extra.shape[0])
            x = near[pl.ds(i * CHUNK * heads, CHUNK * heads), :].reshape(CHUNK, heads, width)
            if extra is not None:
                x = x + repeat_rows(extra, 2)
            out[pl.ds(i * CHUNK, CHUNK)] = x.astype(BF16)
        return carry

    lax.fori_loop(0, chunks, finish_kv, 0)

    for copy in sends + [first] + list(forwards.values()) + list(halves.values()):
        copy.wait_send()
    for copy in [first_back] + returns:
        copy.wait_send()


def hand_over(*refs):
    copies = [pltpu.make_async_copy(refs[i], refs[4 + i], refs[8].at[i]) for i in range(4)]
    for copy in copies:
        copy.start()
    for copy in copies:
        copy.wait()


def on_device(query_rows, key_rows, value_rows, out_grad):
    rows, heads, width = query_rows.shape
    devices = lax.axis_size("seq")
    levels = (rows * devices // BLOCK).bit_length() - 1
    remote = range(1, levels)
    wide = range(2, levels)
    copies = 1 + sum(1 << (level - 2) for level in wide)
    half = BLOCK // 2

    def kept(level):
        return max(rows >> level, CHUNK)

    flat = (rows * heads, width)
    dma = pltpu.SemaphoreType.DMA
    scratch = [pltpu.VMEM(flat, F32) for _ in range(5)]
    scratch += [pltpu.VMEM((3, CHUNK, heads, width), F32) for _ in range(2)]
    scratch += [pltpu.VMEM((heads, rows, rows), F32), pltpu.VMEM((heads, rows, width), F32)]
    scratch += [pltpu.VMEM((heads, rows, 1), F32) for _ in range(4)]
    scratch += [dma((copies,)), dma((levels,)), dma((levels,)), dma((levels,))]
    scratch += [dma((levels,)), dma((levels,)), dma((copies,)), dma((levels,))]
    scratch += [pltpu.VMEM((kept(level) * heads, width), F32) for level in remote]
    scratch += [pltpu.VMEM((2, rows >> level, heads, width), BF16) for level in remote]
    scratch += [
        pltpu.VMEM((1, 2, BLOCK, heads, width) if level == 1 else (2, 2, half, heads, width), BF16)
        for level in remote
    ]
    scratch += [pltpu.VMEM((2, BLOCK * heads, width), F32) for level in remote]
    scratch += [
        pltpu.VMEM((2, BLOCK if level == 1 else half, heads, width), BF16) for level in remote
    ]
    for _ in range(2):
        scratch += [
            pltpu.VMEM((2, CHUNK if level == 1 else half, heads, width), BF16) for level in remote
        ]
    scratch += [
        pltpu.VMEM((max(1 << level >> 2, 1), 2, rows >> level, heads, width), BF16)
        for level in remote
    ]
    for depth, kind in ((BLOCK, F32), (1, F32), (1, F32), (width, F32), (width, BF16), (1, F32)):
        scratch += [pltpu.VMEM((heads, kept(level), depth), kind) for level in remote]
    vmem = pl.BlockSpec(memory_space=pltpu.VMEM)
    out = jax.ShapeDtypeStruct(query_rows.shape, BF16)
    made = pl.pallas_call(
        partial(kernel, levels, heads, width, rows),
        out_shape=(out, out, out, out),
        in_specs=[vmem] * 4,
        out_specs=(vmem,) * 4,
        scratch_shapes=scratch,
        compiler_params=pltpu.CompilerParams(
            collective_id=0, has_side_effects=True, vmem_limit_bytes=58 << 20
        ),
    )(query_rows, key_rows, value_rows, out_grad)
    whole = pl.BlockSpec(memory_space=pl.ANY)
    return pl.pallas_call(
        hand_over,
        out_shape=(out, out, out, out),
        in_specs=[whole] * 4,
        out_specs=(whole,) * 4,
        scratch_shapes=[dma((4,))],
    )(*made)


def solution(mesh):
    spec = P(("groups", "seq"), None, None)
    return jax.shard_map(
        on_device,
        mesh=mesh,
        in_specs=(spec,) * 4,
        out_specs=(spec,) * 4,
        check_vma=False,
    )
```

```python
from functools import partial

import jax
import jax.numpy as jnp
from jax import lax
from jax.experimental import pallas as pl
from jax.experimental.pallas import tpu as pltpu
from jax.sharding import PartitionSpec as P

BLOCK = 128
CHUNK = 16
F32 = jnp.float32
BF16 = jnp.bfloat16
MESH = pl.DeviceIdType.MESH


def bit_reversed(value, bits):
    return sum(((value >> bit) & 1) << (bits - 1 - bit) for bit in range(bits))


def load_rows(ref, head, heads, level):
    bits = max(4 - level, 0)
    parts = [
        ref[pl.ds(bit_reversed(b, bits) * heads + head, CHUNK, stride=heads << bits), :]
        for b in range(1 << bits)
    ]
    return parts[0] if len(parts) == 1 else jnp.concatenate(parts, 0)


def store_rows(ref, head, heads, level, values):
    bits = max(4 - level, 0)
    for b in range(1 << bits):
        ref[pl.ds(bit_reversed(b, bits) * heads + head, CHUNK, stride=heads << bits), :] = values[
            b * CHUNK : (b + 1) * CHUNK
        ]


def dot_nt(a, b):
    return lax.dot_general(a, b, (((1,), (1,)), ((), ())), preferred_element_type=F32)


def dot_nn(a, b):
    return lax.dot_general(a, b, (((1,), (0,)), ((), ())), preferred_element_type=F32)


def dot_tn(a, b):
    return lax.dot_general(a, b, (((0,), (0,)), ((), ())), preferred_element_type=F32)


def pair_sum(x):
    return jnp.sum(x.reshape((x.shape[0] // 2, 2) + x.shape[1:]), axis=1)


def repeat_rows(x, times):
    spread = jnp.broadcast_to(x[:, None], (x.shape[0], times) + x.shape[1:])
    return spread.reshape((x.shape[0] * times,) + x.shape[1:])


def kernel(levels, heads, width, rows, *refs):
    q_ref, k_ref, v_ref, g_ref, o_ref, dq_ref, dk_ref, dv_ref = refs[:8]
    (q32, k32, v32, g32, att32, tops, high, p0, num0, m0, l0, c0, d0) = refs[8:21]
    (sem_out, sem_in, sem_fwd_out, sem_fwd_in) = refs[21:25]
    (sem_half_out, sem_half_in, sem_back_out, sem_back_in) = refs[25:29]
    per = levels - 1
    cut = 29
    groups = [dict(zip(range(1, levels), refs[cut + i * per : cut + (i + 1) * per])) for i in range(14)]
    ql, own, got, kv32, give, gain, total, back, pf, mf, lf, numf, gf, df = groups
    factor = width ** (-0.5)
    remote = list(range(1, levels))
    wide = [level for level in remote if level >= 2]
    chunks = rows // CHUNK
    half = BLOCK // 2

    me = lax.axis_index("seq")
    core = me % 2
    sibling = me + 1 - 2 * core

    def partners(level):
        span = 1 << (level - 1)
        block = me // span
        base = (block + 1 - 2 * (block % 2)) * span
        return [base + 2 * j + core for j in range(span // 2)]

    def place(level):
        return (me % (1 << (level - 1))) // 2

    barrier = pltpu.get_barrier_semaphore()
    peers = [sibling] + [peer for level in wide for peer in partners(level)]
    for peer in peers:
        pl.semaphore_signal(barrier, inc=1, device_id={"seq": peer}, device_id_type=MESH)

    def remote_copy(src, dst, send, recv, peer):
        return pltpu.make_async_remote_copy(
            src_ref=src, dst_ref=dst, send_sem=send, recv_sem=recv,
            device_id={"seq": peer}, device_id_type=MESH,
        )

    def prepare_kv(i, carry):
        for which, (ref, store) in enumerate(((k_ref, k32), (v_ref, v32))):
            x = ref[pl.ds(i * CHUNK, CHUNK)].astype(F32)
            store[pl.ds(i * CHUNK * heads, CHUNK * heads), :] = x.reshape(CHUNK * heads, width)
            for level in range(1, min(levels, 5)):
                x = pair_sum(x)
                n = CHUNK >> level
                own[level][which, pl.ds(i * n, n)] = (x * 0.5**level).astype(BF16)
            if levels > 5:
                tops[which, pl.ds(i, 1)] = x
        return carry

    lax.fori_loop(0, chunks, prepare_kv, 0)
    for which in range(2):
        if levels > 5:
            x = tops[which]
            for level in range(5, levels):
                x = pair_sum(x)
                own[level][which] = (x * 0.5**level).astype(BF16)

    pl.semaphore_wait(barrier, len(peers))
    sends = []
    slot = 0
    for level in wide:
        n = rows >> level
        at = place(level) * n
        for peer in partners(level):
            sends.append(
                remote_copy(
                    own[level], got[level].at[core, :, pl.ds(at, n)],
                    sem_out.at[slot], sem_in.at[level], peer,
                )
            )
            sends[-1].start()
            slot += 1
    first = remote_copy(own[1], got[1].at[0], sem_out.at[slot], sem_in.at[1], sibling)
    first.start()

    def prepare_q(i, carry):
        x = q_ref[pl.ds(i * CHUNK, CHUNK)].astype(F32)
        q32[pl.ds(i * CHUNK * heads, CHUNK * heads), :] = x.reshape(CHUNK * heads, width)
        for level in range(1, min(levels, 5)):
            x = pair_sum(x)
            n = CHUNK >> level
            lowered = (x * 0.5**level).astype(BF16).astype(F32)
            ql[level][pl.ds(i * n * heads, n * heads), :] = lowered.reshape(n * heads, width)
        if levels > 5:
            tops[2, pl.ds(i, 1)] = x
        g = g_ref[pl.ds(i * CHUNK, CHUNK)].astype(F32)
        g32[pl.ds(i * CHUNK * heads, CHUNK * heads), :] = g.reshape(CHUNK * heads, width)
        return carry

    lax.fori_loop(0, chunks, prepare_q, 0)
    if levels > 5:
        x = tops[2]
        for level in range(5, levels):
            x = pair_sum(x)
            lowered = repeat_rows((x * 0.5**level).astype(BF16).astype(F32), 1 << (level - 4))
            ql[level][...] = lowered.reshape(CHUNK * heads, width)

    def in_groups(count, body):
        def step(i, carry):
            body([i * count + j for j in range(count)])
            return carry

        lax.fori_loop(0, heads // count, step, 0)

    def near_forward(hs):
        q = [load_rows(q32, h, heads, 0).astype(BF16) for h in hs]
        k = [k32[pl.ds(h, rows, stride=heads), :].astype(BF16) for h in hs]
        v = [v32[pl.ds(h, rows, stride=heads), :].astype(BF16) for h in hs]
        s = [dot_nt(x, y) * factor for x, y in zip(q, k)]
        m = [jnp.max(x, axis=1, keepdims=True) for x in s]
        p = [jnp.exp(x - y) for x, y in zip(s, m)]
        num = [dot_nn(x.astype(BF16), y) for x, y in zip(p, v)]
        for h, x, y, z in zip(hs, p, m, num):
            p0[h] = x
            m0[h] = y
            l0[h] = jnp.sum(x, axis=1, keepdims=True)
            num0[h] = z

    def far_forward(level, hs):
        q = [load_rows(ql[level], h, heads, level).astype(BF16) for h in hs]
        k = [kv32[level][0, pl.ds(h, BLOCK, stride=heads), :].astype(BF16) for h in hs]
        v = [kv32[level][1, pl.ds(h, BLOCK, stride=heads), :].astype(BF16) for h in hs]
        s = [dot_nt(x, y) * factor for x, y in zip(q, k)]
        m = [jnp.max(x, axis=1, keepdims=True) for x in s]
        p = [jnp.exp(x - y) for x, y in zip(s, m)]
        num = [dot_nn(x.astype(BF16), y) for x, y in zip(p, v)]
        for h, x, y, z in zip(hs, p, m, num):
            pf[level][h] = x
            mf[level][h] = y
            lf[level][h] = jnp.sum(x, axis=1, keepdims=True)
            numf[level][h] = z

    in_groups(2, near_forward)

    def widen(level):
        parts = got[level].shape[0]
        depth = BLOCK // parts

        def body(i, carry):
            n = depth // 8
            for part in range(parts):
                for which in range(2):
                    x = got[level][part, which, pl.ds(i * n, n)].astype(F32)
                    kv32[level][which, pl.ds((part * depth + i * n) * heads, n * heads), :] = x.reshape(
                        n * heads, width
                    )
            return carry

        lax.fori_loop(0, 8, body, 0)

    def take(level):
        other = got[level].at[1 - core]
        remote_copy(other, other, sem_fwd_out.at[level], sem_fwd_in.at[level], sibling).wait_recv()
        widen(level)
        in_groups(8, partial(far_forward, level))

    first.wait_recv()
    widen(1)
    in_groups(8, partial(far_forward, 1))

    forwards = {}
    order = wide
    for step, level in enumerate(order):
        mine = got[level].at[core]
        remote_copy(mine, mine, sem_out.at[0], sem_in.at[level], sibling).wait_recv()
        forwards[level] = remote_copy(
            mine, mine, sem_fwd_out.at[level], sem_fwd_in.at[level], sibling
        )
        forwards[level].start()
        if step:
            take(order[step - 1])
    if order:
        take(order[-1])

    def merge(hs):
        for h in hs:
            state = None
            scales = {}
            for level in reversed(range(levels)):
                if level:
                    m, den_l, num_l = mf[level][h], lf[level][h], numf[level][h]
                else:
                    m, den_l, num_l = m0[h], l0[h], num0[h]
                weight = float(1 << level)
                if state is None:
                    scale_a, scale_b = None, jnp.full(m.shape, weight, F32)
                    state = (m, den_l * weight, num_l * weight)
                else:
                    if state[0].shape[0] < m.shape[0]:
                        state = tuple(jnp.concatenate([x, x], 0) for x in state)
                    top = jnp.maximum(state[0], m)
                    scale_a = jnp.exp(state[0] - top)
                    scale_b = jnp.exp(m - top) * weight
                    state = (
                        top,
                        scale_a * state[1] + scale_b * den_l,
                        scale_a * state[2] + scale_b * num_l,
                    )
                scales[level] = (scale_a, scale_b)
            inverse = 1.0 / state[1]
            att = state[2] * inverse
            store_rows(att32, h, heads, 0, att)
            g = load_rows(g32, h, heads, 0)
            d = jnp.sum(g * att, axis=1, keepdims=True)
            c0[h] = scales[0][1] * inverse
            d0[h] = d
            if levels == 1:
                continue
            scale = scales[0][0] * inverse
            up, up_d = g * scale, d * scale
            for level in remote:
                scale_a, scale_b = scales[level]
                if up.shape[0] > scale_b.shape[0]:
                    n = scale_b.shape[0]
                    up, up_d = up[:n] + up[n:], up_d[:n] + up_d[n:]
                gf[level][h] = (up * scale_b).astype(BF16)
                df[level][h] = up_d * scale_b
                if scale_a is not None:
                    up, up_d = up * scale_a, up_d * scale_a

    in_groups(2, merge)

    def far_backward(level, hs):
        q = [load_rows(ql[level], h, heads, level).astype(BF16) for h in hs]
        k = [kv32[level][0, pl.ds(h, BLOCK, stride=heads), :].astype(BF16) for h in hs]
        v = [kv32[level][1, pl.ds(h, BLOCK, stride=heads), :].astype(BF16) for h in hs]
        p = [pf[level][h] for h in hs]
        g = [gf[level][h] for h in hs]
        d = [df[level][h] for h in hs]
        dp = [dot_nt(x, y) for x, y in zip(g, v)]
        ds = [(x * (y - z) * factor).astype(BF16) for x, y, z in zip(p, dp, d)]
        dv = [dot_tn(x.astype(BF16), y) for x, y in zip(p, g)]
        dq = [dot_nn(x, y) for x, y in zip(ds, k)]
        dk = [dot_tn(x, y) for x, y in zip(ds, q)]
        for h, x, y, z in zip(hs, dq, dk, dv):
            store_rows(ql[level], h, heads, level, x)
            kv32[level][0, pl.ds(h, BLOCK, stride=heads), :] = y
            kv32[level][1, pl.ds(h, BLOCK, stride=heads), :] = z

    halves = {}
    returns = []

    def leave(level):
        in_groups(8, partial(far_backward, level))

        def narrow(i, carry):
            n = half // 4
            for which in range(2):
                x = kv32[level][which, pl.ds(((1 - core) * half + i * n) * heads, n * heads), :]
                give[level][which, pl.ds(i * n, n)] = x.reshape(n, heads, width).astype(BF16)
            return carry

        lax.fori_loop(0, 4, narrow, 0)
        halves[level] = remote_copy(
            give[level], gain[level], sem_half_out.at[level], sem_half_in.at[level], sibling
        )
        halves[level].start()

    def pass_on(level):
        halves[level].wait_recv()

        def add(i, carry):
            n = half // 4
            for which in range(2):
                x = kv32[level][which, pl.ds((core * half + i * n) * heads, n * heads), :]
                y = gain[level][which, pl.ds(i * n, n)].astype(F32)
                total[level][which, pl.ds(i * n, n)] = (x.reshape(n, heads, width) + y).astype(BF16)
            return carry

        lax.fori_loop(0, 4, add, 0)
        n = rows >> level
        for j, peer in enumerate(partners(level)):
            returns.append(
                remote_copy(
                    total[level].at[:, pl.ds(j * n, n)], back[level].at[place(level)],
                    sem_back_out.at[len(returns)], sem_back_in.at[level], peer,
                )
            )
            returns[-1].start()

    for step, level in enumerate(wide):
        leave(level)
        if step:
            pass_on(wide[step - 1])
    in_groups(8, partial(far_backward, 1))

    def narrow_first(i, carry):
        n = BLOCK // 8
        for which in range(2):
            x = kv32[1][which, pl.ds(i * n * heads, n * heads), :]
            give[1][which, pl.ds(i * n, n)] = x.reshape(n, heads, width).astype(BF16)
        return carry

    if wide:
        pass_on(wide[-1])
    lax.fori_loop(0, 8, narrow_first, 0)
    first_back = remote_copy(
        give[1], back[1].at[0], sem_half_out.at[1], sem_back_in.at[1], sibling
    )
    first_back.start()

    def near_backward(hs):
        q = [load_rows(q32, h, heads, 0).astype(BF16) for h in hs]
        g = [load_rows(g32, h, heads, 0).astype(BF16) for h in hs]
        k = [k32[pl.ds(h, rows, stride=heads), :].astype(BF16) for h in hs]
        v = [v32[pl.ds(h, rows, stride=heads), :].astype(BF16) for h in hs]
        p = [p0[h] * c0[h] for h in hs]
        dp = [dot_nt(x, y) for x, y in zip(g, v)]
        ds = [(x * (y - d0[h]) * factor).astype(BF16) for x, y, h in zip(p, dp, hs)]
        dv = [dot_tn(x.astype(BF16), y) for x, y in zip(p, g)]
        dq = [dot_nn(x, y) for x, y in zip(ds, k)]
        dk = [dot_tn(x, y) for x, y in zip(ds, q)]
        for h, x, y, z in zip(hs, dq, dk, dv):
            store_rows(q32, h, heads, 0, x)
            k32[pl.ds(h, rows, stride=heads), :] = y
            v32[pl.ds(h, rows, stride=heads), :] = z

    in_groups(2, near_backward)

    low = range(1, min(levels, 5))

    def finish_q(i, carry):
        o = att32[pl.ds(i * CHUNK * heads, CHUNK * heads), :]
        o_ref[pl.ds(i * CHUNK, CHUNK)] = o.reshape(CHUNK, heads, width).astype(BF16)
        extra = high[0, pl.ds(i, 1)] if levels > 5 else None
        for level in reversed(low):
            n = CHUNK >> level
            x = ql[level][pl.ds(i * n * heads, n * heads), :].reshape(n, heads, width) * 0.5**level
            extra = x if extra is None else x + repeat_rows(extra, n // extra.shape[0])
        x = q32[pl.ds(i * CHUNK * heads, CHUNK * heads), :].reshape(CHUNK, heads, width)
        if extra is not None:
            x = x + repeat_rows(extra, 2)
        dq_ref[pl.ds(i * CHUNK, CHUNK)] = x.astype(BF16)
        return carry

    if levels > 5:
        total_q = jnp.zeros((CHUNK, heads, width), F32)
        for level in range(5, levels):
            x = ql[level][...].reshape(CHUNK, heads, width)
            for _ in range(level - 4):
                x = pair_sum(x)
            total_q = total_q + repeat_rows(x * 0.5**level, 1 << (level - 4))
        high[0] = total_q
    lax.fori_loop(0, chunks, finish_q, 0)

    first_back.wait_recv()
    for level in wide:
        remote_copy(
            back[level], back[level], sem_back_out.at[0], sem_back_in.at[level], sibling
        ).wait_recv()

    if levels > 5:
        for which in range(2):
            total_k = jnp.zeros((CHUNK, heads, width), F32)
            for level in range(5, levels):
                x = back[level][0, which].astype(F32)
                for j in range(1, back[level].shape[0]):
                    x = x + back[level][j, which].astype(F32)
                total_k = total_k + repeat_rows(x * 0.5**level, 1 << (level - 4))
            high[1 + which] = total_k

    def finish_kv(i, carry):
        for which, (near, out) in enumerate(((k32, dk_ref), (v32, dv_ref))):
            extra = high[1 + which, pl.ds(i, 1)] if levels > 5 else None
            for level in reversed(low):
                n = CHUNK >> level
                x = back[level][0, which, pl.ds(i * n, n)].astype(F32)
                for j in range(1, back[level].shape[0]):
                    x = x + back[level][j, which, pl.ds(i * n, n)].astype(F32)
                x = x * 0.5**level
                extra = x if extra is None else x + repeat_rows(extra, n // extra.shape[0])
            x = near[pl.ds(i * CHUNK * heads, CHUNK * heads), :].reshape(CHUNK, heads, width)
            if extra is not None:
                x = x + repeat_rows(extra, 2)
            out[pl.ds(i * CHUNK, CHUNK)] = x.astype(BF16)
        return carry

    lax.fori_loop(0, chunks, finish_kv, 0)

    for copy in sends + [first] + list(forwards.values()) + list(halves.values()):
        copy.wait_send()
    for copy in [first_back] + returns:
        copy.wait_send()


def hand_over(*refs):
    given, made, held = refs[:4], refs[4:8], refs[8:12]
    arrive, leave = refs[12:]
    inward = [pltpu.make_async_copy(given[i], held[i], arrive.at[i]) for i in range(4)]
    outward = [pltpu.make_async_copy(held[i], made[i], leave.at[i]) for i in range(4)]
    for copy in inward:
        copy.start()
    for i in range(4):
        inward[i].wait()
        outward[i].start()
    for copy in outward:
        copy.wait()


def on_device(query_rows, key_rows, value_rows, out_grad):
    rows, heads, width = query_rows.shape
    devices = lax.axis_size("seq")
    levels = (rows * devices // BLOCK).bit_length() - 1
    remote = range(1, levels)
    wide = range(2, levels)
    copies = 1 + sum(1 << (level - 2) for level in wide)
    half = BLOCK // 2

    def kept(level):
        return max(rows >> level, CHUNK)

    flat = (rows * heads, width)
    dma = pltpu.SemaphoreType.DMA
    scratch = [pltpu.VMEM(flat, F32) for _ in range(5)]
    scratch += [pltpu.VMEM((3, CHUNK, heads, width), F32) for _ in range(2)]
    scratch += [pltpu.VMEM((heads, rows, rows), F32), pltpu.VMEM((heads, rows, width), F32)]
    scratch += [pltpu.VMEM((heads, rows, 1), F32) for _ in range(4)]
    scratch += [dma((copies,)), dma((levels,)), dma((levels,)), dma((levels,))]
    scratch += [dma((levels,)), dma((levels,)), dma((copies,)), dma((levels,))]
    scratch += [pltpu.VMEM((kept(level) * heads, width), F32) for level in remote]
    scratch += [pltpu.VMEM((2, rows >> level, heads, width), BF16) for level in remote]
    scratch += [
        pltpu.VMEM((1, 2, BLOCK, heads, width) if level == 1 else (2, 2, half, heads, width), BF16)
        for level in remote
    ]
    scratch += [pltpu.VMEM((2, BLOCK * heads, width), F32) for level in remote]
    scratch += [
        pltpu.VMEM((2, BLOCK if level == 1 else half, heads, width), BF16) for level in remote
    ]
    for _ in range(2):
        scratch += [
            pltpu.VMEM((2, CHUNK if level == 1 else half, heads, width), BF16) for level in remote
        ]
    scratch += [
        pltpu.VMEM((max(1 << level >> 2, 1), 2, rows >> level, heads, width), BF16)
        for level in remote
    ]
    for depth, kind in ((BLOCK, F32), (1, F32), (1, F32), (width, F32), (width, BF16), (1, F32)):
        scratch += [pltpu.VMEM((heads, kept(level), depth), kind) for level in remote]
    vmem = pl.BlockSpec(memory_space=pltpu.VMEM)
    out = jax.ShapeDtypeStruct(query_rows.shape, BF16)
    made = pl.pallas_call(
        partial(kernel, levels, heads, width, rows),
        out_shape=(out, out, out, out),
        in_specs=[vmem] * 4,
        out_specs=(vmem,) * 4,
        scratch_shapes=scratch,
        compiler_params=pltpu.CompilerParams(
            collective_id=0, has_side_effects=True, vmem_limit_bytes=58 << 20
        ),
    )(query_rows, key_rows, value_rows, out_grad)
    whole = pl.BlockSpec(memory_space=pl.ANY)
    return pl.pallas_call(
        hand_over,
        out_shape=(out, out, out, out),
        in_specs=[whole] * 4,
        out_specs=(whole,) * 4,
        scratch_shapes=[pltpu.VMEM(query_rows.shape, BF16) for _ in range(4)] + [dma((4,)), dma((4,))],
    )(*made)


def solution(mesh):
    spec = P(("groups", "seq"), None, None)
    return jax.shard_map(
        on_device,
        mesh=mesh,
        in_specs=(spec,) * 4,
        out_specs=(spec,) * 4,
        check_vma=False,
    )
```

```python
from functools import partial

import jax
import jax.numpy as jnp
from jax import lax
from jax.experimental import pallas as pl
from jax.experimental.pallas import tpu as pltpu
from jax.sharding import PartitionSpec as P

BLOCK = 128
CHUNK = 16
F32 = jnp.float32
BF16 = jnp.bfloat16
MESH = pl.DeviceIdType.MESH


def bit_reversed(value, bits):
    return sum(((value >> bit) & 1) << (bits - 1 - bit) for bit in range(bits))


def load_rows(ref, head, heads, level):
    bits = max(4 - level, 0)
    parts = [
        ref[pl.ds(bit_reversed(b, bits) * heads + head, CHUNK, stride=heads << bits), :]
        for b in range(1 << bits)
    ]
    return parts[0] if len(parts) == 1 else jnp.concatenate(parts, 0)


def store_rows(ref, head, heads, level, values):
    bits = max(4 - level, 0)
    for b in range(1 << bits):
        ref[pl.ds(bit_reversed(b, bits) * heads + head, CHUNK, stride=heads << bits), :] = values[
            b * CHUNK : (b + 1) * CHUNK
        ]


def dot_nt(a, b):
    return lax.dot_general(a, b, (((1,), (1,)), ((), ())), preferred_element_type=F32)


def dot_nn(a, b):
    return lax.dot_general(a, b, (((1,), (0,)), ((), ())), preferred_element_type=F32)


def dot_tn(a, b):
    return lax.dot_general(a, b, (((0,), (0,)), ((), ())), preferred_element_type=F32)


def pair_sum(x):
    return jnp.sum(x.reshape((x.shape[0] // 2, 2) + x.shape[1:]), axis=1)


def repeat_rows(x, times):
    spread = jnp.broadcast_to(x[:, None], (x.shape[0], times) + x.shape[1:])
    return spread.reshape((x.shape[0] * times,) + x.shape[1:])


def kernel(levels, heads, width, rows, *refs):
    q_ref, k_ref, v_ref, g_ref, o_ref, dq_ref, dk_ref, dv_ref = refs[:8]
    q_hbm, g_hbm, o_hbm, dq_hbm = q_ref, g_ref, o_ref, dq_ref
    q_ref, g_ref, o_ref, dq_ref, sem_local = refs[-5:]
    fetch_q = pltpu.make_async_copy(q_hbm, q_ref, sem_local.at[0])
    fetch_g = pltpu.make_async_copy(g_hbm, g_ref, sem_local.at[1])
    fetch_q.start()
    fetch_g.start()
    (q32, k32, v32, g32, att32, tops, high, p0, num0, m0, l0, c0, d0) = refs[8:21]
    (sem_out, sem_in, sem_fwd_out, sem_fwd_in) = refs[21:25]
    (sem_half_out, sem_half_in, sem_back_out, sem_back_in) = refs[25:29]
    per = levels - 1
    cut = 29
    groups = [dict(zip(range(1, levels), refs[cut + i * per : cut + (i + 1) * per])) for i in range(14)]
    ql, own, got, kv32, give, gain, total, back, pf, mf, lf, numf, gf, df = groups
    factor = width ** (-0.5)
    remote = list(range(1, levels))
    wide = [level for level in remote if level >= 2]
    chunks = rows // CHUNK
    half = BLOCK // 2

    me = lax.axis_index("seq")
    core = me % 2
    sibling = me + 1 - 2 * core

    def partners(level):
        span = 1 << (level - 1)
        block = me // span
        base = (block + 1 - 2 * (block % 2)) * span
        return [base + 2 * j + core for j in range(span // 2)]

    def place(level):
        return (me % (1 << (level - 1))) // 2

    barrier = pltpu.get_barrier_semaphore()
    peers = [sibling] + [peer for level in wide for peer in partners(level)]
    for peer in peers:
        pl.semaphore_signal(barrier, inc=1, device_id={"seq": peer}, device_id_type=MESH)

    def remote_copy(src, dst, send, recv, peer):
        return pltpu.make_async_remote_copy(
            src_ref=src, dst_ref=dst, send_sem=send, recv_sem=recv,
            device_id={"seq": peer}, device_id_type=MESH,
        )

    def prepare_kv(i, carry):
        for which, (ref, store) in enumerate(((k_ref, k32), (v_ref, v32))):
            x = ref[pl.ds(i * CHUNK, CHUNK)].astype(F32)
            store[pl.ds(i * CHUNK * heads, CHUNK * heads), :] = x.reshape(CHUNK * heads, width)
            for level in range(1, min(levels, 5)):
                x = pair_sum(x)
                n = CHUNK >> level
                own[level][which, pl.ds(i * n, n)] = (x * 0.5**level).astype(BF16)
            if levels > 5:
                tops[which, pl.ds(i, 1)] = x
        return carry

    lax.fori_loop(0, chunks, prepare_kv, 0)
    for which in range(2):
        if levels > 5:
            x = tops[which]
            for level in range(5, levels):
                x = pair_sum(x)
                own[level][which] = (x * 0.5**level).astype(BF16)

    pl.semaphore_wait(barrier, len(peers))
    sends = []
    slot = 0
    for level in wide:
        n = rows >> level
        at = place(level) * n
        for peer in partners(level):
            sends.append(
                remote_copy(
                    own[level], got[level].at[core, :, pl.ds(at, n)],
                    sem_out.at[slot], sem_in.at[level], peer,
                )
            )
            sends[-1].start()
            slot += 1
    first = remote_copy(own[1], got[1].at[0], sem_out.at[slot], sem_in.at[1], sibling)
    first.start()

    def prepare_q(i, carry):
        x = q_ref[pl.ds(i * CHUNK, CHUNK)].astype(F32)
        q32[pl.ds(i * CHUNK * heads, CHUNK * heads), :] = x.reshape(CHUNK * heads, width)
        for level in range(1, min(levels, 5)):
            x = pair_sum(x)
            n = CHUNK >> level
            lowered = (x * 0.5**level).astype(BF16).astype(F32)
            ql[level][pl.ds(i * n * heads, n * heads), :] = lowered.reshape(n * heads, width)
        if levels > 5:
            tops[2, pl.ds(i, 1)] = x
        g = g_ref[pl.ds(i * CHUNK, CHUNK)].astype(F32)
        g32[pl.ds(i * CHUNK * heads, CHUNK * heads), :] = g.reshape(CHUNK * heads, width)
        return carry

    fetch_q.wait()
    fetch_g.wait()
    lax.fori_loop(0, chunks, prepare_q, 0)
    if levels > 5:
        x = tops[2]
        for level in range(5, levels):
            x = pair_sum(x)
            lowered = repeat_rows((x * 0.5**level).astype(BF16).astype(F32), 1 << (level - 4))
            ql[level][...] = lowered.reshape(CHUNK * heads, width)

    def in_groups(count, body):
        def step(i, carry):
            body([i * count + j for j in range(count)])
            return carry

        lax.fori_loop(0, heads // count, step, 0)

    def near_forward(hs):
        q = [load_rows(q32, h, heads, 0).astype(BF16) for h in hs]
        k = [k32[pl.ds(h, rows, stride=heads), :].astype(BF16) for h in hs]
        v = [v32[pl.ds(h, rows, stride=heads), :].astype(BF16) for h in hs]
        s = [dot_nt(x, y) * factor for x, y in zip(q, k)]
        m = [jnp.max(x, axis=1, keepdims=True) for x in s]
        p = [jnp.exp(x - y) for x, y in zip(s, m)]
        num = [dot_nn(x.astype(BF16), y) for x, y in zip(p, v)]
        for h, x, y, z in zip(hs, p, m, num):
            p0[h] = x
            m0[h] = y
            l0[h] = jnp.sum(x, axis=1, keepdims=True)
            num0[h] = z

    def far_forward(level, hs):
        q = [load_rows(ql[level], h, heads, level).astype(BF16) for h in hs]
        k = [kv32[level][0, pl.ds(h, BLOCK, stride=heads), :].astype(BF16) for h in hs]
        v = [kv32[level][1, pl.ds(h, BLOCK, stride=heads), :].astype(BF16) for h in hs]
        s = [dot_nt(x, y) * factor for x, y in zip(q, k)]
        m = [jnp.max(x, axis=1, keepdims=True) for x in s]
        p = [jnp.exp(x - y) for x, y in zip(s, m)]
        num = [dot_nn(x.astype(BF16), y) for x, y in zip(p, v)]
        for h, x, y, z in zip(hs, p, m, num):
            pf[level][h] = x
            mf[level][h] = y
            lf[level][h] = jnp.sum(x, axis=1, keepdims=True)
            numf[level][h] = z

    in_groups(2, near_forward)

    def widen(level):
        parts = got[level].shape[0]
        depth = BLOCK // parts

        def body(i, carry):
            n = depth // 8
            for part in range(parts):
                for which in range(2):
                    x = got[level][part, which, pl.ds(i * n, n)].astype(F32)
                    kv32[level][which, pl.ds((part * depth + i * n) * heads, n * heads), :] = x.reshape(
                        n * heads, width
                    )
            return carry

        lax.fori_loop(0, 8, body, 0)

    def take(level):
        other = got[level].at[1 - core]
        remote_copy(other, other, sem_fwd_out.at[level], sem_fwd_in.at[level], sibling).wait_recv()
        widen(level)
        in_groups(8, partial(far_forward, level))

    first.wait_recv()
    widen(1)
    in_groups(8, partial(far_forward, 1))

    forwards = {}
    order = wide
    for step, level in enumerate(order):
        mine = got[level].at[core]
        remote_copy(mine, mine, sem_out.at[0], sem_in.at[level], sibling).wait_recv()
        forwards[level] = remote_copy(
            mine, mine, sem_fwd_out.at[level], sem_fwd_in.at[level], sibling
        )
        forwards[level].start()
        if step:
            take(order[step - 1])
    if order:
        take(order[-1])

    def merge(hs):
        for h in hs:
            state = None
            scales = {}
            for level in reversed(range(levels)):
                if level:
                    m, den_l, num_l = mf[level][h], lf[level][h], numf[level][h]
                else:
                    m, den_l, num_l = m0[h], l0[h], num0[h]
                weight = float(1 << level)
                if state is None:
                    scale_a, scale_b = None, jnp.full(m.shape, weight, F32)
                    state = (m, den_l * weight, num_l * weight)
                else:
                    if state[0].shape[0] < m.shape[0]:
                        state = tuple(jnp.concatenate([x, x], 0) for x in state)
                    top = jnp.maximum(state[0], m)
                    scale_a = jnp.exp(state[0] - top)
                    scale_b = jnp.exp(m - top) * weight
                    state = (
                        top,
                        scale_a * state[1] + scale_b * den_l,
                        scale_a * state[2] + scale_b * num_l,
                    )
                scales[level] = (scale_a, scale_b)
            inverse = 1.0 / state[1]
            att = state[2] * inverse
            store_rows(att32, h, heads, 0, att)
            g = load_rows(g32, h, heads, 0)
            d = jnp.sum(g * att, axis=1, keepdims=True)
            c0[h] = scales[0][1] * inverse
            d0[h] = d
            if levels == 1:
                continue
            scale = scales[0][0] * inverse
            up, up_d = g * scale, d * scale
            for level in remote:
                scale_a, scale_b = scales[level]
                if up.shape[0] > scale_b.shape[0]:
                    n = scale_b.shape[0]
                    up, up_d = up[:n] + up[n:], up_d[:n] + up_d[n:]
                gf[level][h] = (up * scale_b).astype(BF16)
                df[level][h] = up_d * scale_b
                if scale_a is not None:
                    up, up_d = up * scale_a, up_d * scale_a

    in_groups(4, merge)

    def far_backward(level, hs):
        q = [load_rows(ql[level], h, heads, level).astype(BF16) for h in hs]
        k = [kv32[level][0, pl.ds(h, BLOCK, stride=heads), :].astype(BF16) for h in hs]
        v = [kv32[level][1, pl.ds(h, BLOCK, stride=heads), :].astype(BF16) for h in hs]
        p = [pf[level][h] for h in hs]
        g = [gf[level][h] for h in hs]
        d = [df[level][h] for h in hs]
        dp = [dot_nt(x, y) for x, y in zip(g, v)]
        ds = [(x * (y - z) * factor).astype(BF16) for x, y, z in zip(p, dp, d)]
        dv = [dot_tn(x.astype(BF16), y) for x, y in zip(p, g)]
        dq = [dot_nn(x, y) for x, y in zip(ds, k)]
        dk = [dot_tn(x, y) for x, y in zip(ds, q)]
        for h, x, y, z in zip(hs, dq, dk, dv):
            store_rows(ql[level], h, heads, level, x)
            kv32[level][0, pl.ds(h, BLOCK, stride=heads), :] = y
            kv32[level][1, pl.ds(h, BLOCK, stride=heads), :] = z

    halves = {}
    returns = []

    def leave(level):
        in_groups(8, partial(far_backward, level))

        def narrow(i, carry):
            n = half // 4
            for which in range(2):
                x = kv32[level][which, pl.ds(((1 - core) * half + i * n) * heads, n * heads), :]
                give[level][which, pl.ds(i * n, n)] = x.reshape(n, heads, width).astype(BF16)
            return carry

        lax.fori_loop(0, 4, narrow, 0)
        halves[level] = remote_copy(
            give[level], gain[level], sem_half_out.at[level], sem_half_in.at[level], sibling
        )
        halves[level].start()

    def pass_on(level):
        halves[level].wait_recv()

        def add(i, carry):
            n = half // 4
            for which in range(2):
                x = kv32[level][which, pl.ds((core * half + i * n) * heads, n * heads), :]
                y = gain[level][which, pl.ds(i * n, n)].astype(F32)
                total[level][which, pl.ds(i * n, n)] = (x.reshape(n, heads, width) + y).astype(BF16)
            return carry

        lax.fori_loop(0, 4, add, 0)
        n = rows >> level
        for j, peer in enumerate(partners(level)):
            returns.append(
                remote_copy(
                    total[level].at[:, pl.ds(j * n, n)], back[level].at[place(level)],
                    sem_back_out.at[len(returns)], sem_back_in.at[level], peer,
                )
            )
            returns[-1].start()

    for step, level in enumerate(wide):
        leave(level)
        if step:
            pass_on(wide[step - 1])
    in_groups(8, partial(far_backward, 1))

    def narrow_first(i, carry):
        n = BLOCK // 8
        for which in range(2):
            x = kv32[1][which, pl.ds(i * n * heads, n * heads), :]
            give[1][which, pl.ds(i * n, n)] = x.reshape(n, heads, width).astype(BF16)
        return carry

    if wide:
        pass_on(wide[-1])
    lax.fori_loop(0, 8, narrow_first, 0)
    first_back = remote_copy(
        give[1], back[1].at[0], sem_half_out.at[1], sem_back_in.at[1], sibling
    )
    first_back.start()

    def near_backward(hs):
        q = [load_rows(q32, h, heads, 0).astype(BF16) for h in hs]
        g = [load_rows(g32, h, heads, 0).astype(BF16) for h in hs]
        k = [k32[pl.ds(h, rows, stride=heads), :].astype(BF16) for h in hs]
        v = [v32[pl.ds(h, rows, stride=heads), :].astype(BF16) for h in hs]
        p = [p0[h] * c0[h] for h in hs]
        dp = [dot_nt(x, y) for x, y in zip(g, v)]
        ds = [(x * (y - d0[h]) * factor).astype(BF16) for x, y, h in zip(p, dp, hs)]
        dv = [dot_tn(x.astype(BF16), y) for x, y in zip(p, g)]
        dq = [dot_nn(x, y) for x, y in zip(ds, k)]
        dk = [dot_tn(x, y) for x, y in zip(ds, q)]
        for h, x, y, z in zip(hs, dq, dk, dv):
            store_rows(q32, h, heads, 0, x)
            k32[pl.ds(h, rows, stride=heads), :] = y
            v32[pl.ds(h, rows, stride=heads), :] = z

    in_groups(2, near_backward)

    low = range(1, min(levels, 5))

    def finish_q(i, carry):
        o = att32[pl.ds(i * CHUNK * heads, CHUNK * heads), :]
        o_ref[pl.ds(i * CHUNK, CHUNK)] = o.reshape(CHUNK, heads, width).astype(BF16)
        extra = high[0, pl.ds(i, 1)] if levels > 5 else None
        for level in reversed(low):
            n = CHUNK >> level
            x = ql[level][pl.ds(i * n * heads, n * heads), :].reshape(n, heads, width) * 0.5**level
            extra = x if extra is None else x + repeat_rows(extra, n // extra.shape[0])
        x = q32[pl.ds(i * CHUNK * heads, CHUNK * heads), :].reshape(CHUNK, heads, width)
        if extra is not None:
            x = x + repeat_rows(extra, 2)
        dq_ref[pl.ds(i * CHUNK, CHUNK)] = x.astype(BF16)
        return carry

    if levels > 5:
        total_q = jnp.zeros((CHUNK, heads, width), F32)
        for level in range(5, levels):
            x = ql[level][...].reshape(CHUNK, heads, width)
            for _ in range(level - 4):
                x = pair_sum(x)
            total_q = total_q + repeat_rows(x * 0.5**level, 1 << (level - 4))
        high[0] = total_q
    lax.fori_loop(0, chunks, finish_q, 0)
    store_o = pltpu.make_async_copy(o_ref, o_hbm, sem_local.at[2])
    store_q = pltpu.make_async_copy(dq_ref, dq_hbm, sem_local.at[3])
    store_o.start()
    store_q.start()

    first_back.wait_recv()
    for level in wide:
        remote_copy(
            back[level], back[level], sem_back_out.at[0], sem_back_in.at[level], sibling
        ).wait_recv()

    if levels > 5:
        for which in range(2):
            total_k = jnp.zeros((CHUNK, heads, width), F32)
            for level in range(5, levels):
                x = back[level][0, which].astype(F32)
                for j in range(1, back[level].shape[0]):
                    x = x + back[level][j, which].astype(F32)
                total_k = total_k + repeat_rows(x * 0.5**level, 1 << (level - 4))
            high[1 + which] = total_k

    def finish_kv(i, carry):
        for which, (near, out) in enumerate(((k32, dk_ref), (v32, dv_ref))):
            extra = high[1 + which, pl.ds(i, 1)] if levels > 5 else None
            for level in reversed(low):
                n = CHUNK >> level
                x = back[level][0, which, pl.ds(i * n, n)].astype(F32)
                for j in range(1, back[level].shape[0]):
                    x = x + back[level][j, which, pl.ds(i * n, n)].astype(F32)
                x = x * 0.5**level
                extra = x if extra is None else x + repeat_rows(extra, n // extra.shape[0])
            x = near[pl.ds(i * CHUNK * heads, CHUNK * heads), :].reshape(CHUNK, heads, width)
            if extra is not None:
                x = x + repeat_rows(extra, 2)
            out[pl.ds(i * CHUNK, CHUNK)] = x.astype(BF16)
        return carry

    lax.fori_loop(0, chunks, finish_kv, 0)

    store_o.wait()
    store_q.wait()
    for copy in sends + [first] + list(forwards.values()) + list(halves.values()):
        copy.wait_send()
    for copy in [first_back] + returns:
        copy.wait_send()


def hand_over(*refs):
    given, made, held = refs[:4], refs[4:8], refs[8:12]
    arrive, leave = refs[12:]
    inward = [pltpu.make_async_copy(given[i], held[i], arrive.at[i]) for i in range(4)]
    outward = [pltpu.make_async_copy(held[i], made[i], leave.at[i]) for i in range(4)]
    for copy in inward:
        copy.start()
    for i in range(4):
        inward[i].wait()
        outward[i].start()
    for copy in outward:
        copy.wait()


def on_device(query_rows, key_rows, value_rows, out_grad):
    rows, heads, width = query_rows.shape
    devices = lax.axis_size("seq")
    levels = (rows * devices // BLOCK).bit_length() - 1
    remote = range(1, levels)
    wide = range(2, levels)
    copies = 1 + sum(1 << (level - 2) for level in wide)
    half = BLOCK // 2

    def kept(level):
        return max(rows >> level, CHUNK)

    flat = (rows * heads, width)
    dma = pltpu.SemaphoreType.DMA
    scratch = [pltpu.VMEM(flat, F32) for _ in range(5)]
    scratch += [pltpu.VMEM((3, CHUNK, heads, width), F32) for _ in range(2)]
    scratch += [pltpu.VMEM((heads, rows, rows), F32), pltpu.VMEM((heads, rows, width), F32)]
    scratch += [pltpu.VMEM((heads, rows, 1), F32) for _ in range(4)]
    scratch += [dma((copies,)), dma((levels,)), dma((levels,)), dma((levels,))]
    scratch += [dma((levels,)), dma((levels,)), dma((copies,)), dma((levels,))]
    scratch += [pltpu.VMEM((kept(level) * heads, width), F32) for level in remote]
    scratch += [pltpu.VMEM((2, rows >> level, heads, width), BF16) for level in remote]
    scratch += [
        pltpu.VMEM((1, 2, BLOCK, heads, width) if level == 1 else (2, 2, half, heads, width), BF16)
        for level in remote
    ]
    scratch += [pltpu.VMEM((2, BLOCK * heads, width), F32) for level in remote]
    scratch += [
        pltpu.VMEM((2, BLOCK if level == 1 else half, heads, width), BF16) for level in remote
    ]
    for _ in range(2):
        scratch += [
            pltpu.VMEM((2, CHUNK if level == 1 else half, heads, width), BF16) for level in remote
        ]
    scratch += [
        pltpu.VMEM((max(1 << level >> 2, 1), 2, rows >> level, heads, width), BF16)
        for level in remote
    ]
    for depth, kind in ((BLOCK, F32), (1, F32), (1, F32), (width, F32), (width, BF16), (1, F32)):
        scratch += [pltpu.VMEM((heads, kept(level), depth), kind) for level in remote]
    scratch += [pltpu.VMEM(query_rows.shape, BF16) for _ in range(4)] + [dma((4,))]
    vmem = pl.BlockSpec(memory_space=pltpu.VMEM)
    whole = pl.BlockSpec(memory_space=pl.ANY)
    out = jax.ShapeDtypeStruct(query_rows.shape, BF16)
    made = pl.pallas_call(
        partial(kernel, levels, heads, width, rows),
        out_shape=(out, out, out, out),
        in_specs=[whole, vmem, vmem, whole],
        out_specs=(whole, whole, vmem, vmem),
        scratch_shapes=scratch,
        compiler_params=pltpu.CompilerParams(
            collective_id=0, has_side_effects=True, vmem_limit_bytes=58 << 20
        ),
    )(query_rows, key_rows, value_rows, out_grad)
    whole = pl.BlockSpec(memory_space=pl.ANY)
    return pl.pallas_call(
        hand_over,
        out_shape=(out, out, out, out),
        in_specs=[whole] * 4,
        out_specs=(whole,) * 4,
        scratch_shapes=[pltpu.VMEM(query_rows.shape, BF16) for _ in range(4)] + [dma((4,)), dma((4,))],
    )(*made)


def solution(mesh):
    spec = P(("groups", "seq"), None, None)
    return jax.shard_map(
        on_device,
        mesh=mesh,
        in_specs=(spec,) * 4,
        out_specs=(spec,) * 4,
        check_vma=False,
    )
```
